32 devices in a mesh: ingest: 4 (over z), store: 8 (over y, x, core).
Axes of the slice: x: 2, y: 2, z: 4, core: 2. Of those that a mesh axis runs over, the one named last changes fastest.
Arguments:
- counts: int32 [512, 1024], P(('ingest', 'store')), may hold values from 0 to 2047, as said below
- stored: bfloat16 [32768, 1024], P('store'), may hold values from -114 to 114, as said below
- scales: float32 [32768], P('store'), may hold values from 0.018 to 0.056
- col_means: float32 [32768], P('store'), may hold values from 0.05 to 0.45
- eigvecs: float32 [64, 32768], P(None, 'store'), may hold values from -0.03125 to 0.03125
- eigvals: float32 [64], replicated, may hold values from 0.02 to 0.2
Outputs:
- coords: float32 [512, 64], P(('ingest', 'store'))
The draws below stay inside these ranges and needn't reach their ends.
Inputs may be any that keep to these rules, and one draw needn't show every extreme that they name: `counts`: whole numbers. `stored`: whole numbers.
All inputs are finite; a program needn't handle non-finite values.
Results may differ from the reference program's by a relative error of at most 0.00051.
Values may be sent and summed in bfloat16 or wider, within the bound.
A program may use at most 128 MiB of HBM per device.

```python
import math
import jax
import jax.numpy as jnp
from jax import lax

P_SIZE = 1024
NCOORD = 64
STORE_DEV = 4096
BATCH = 512
STORED = 32768
N_STORE = 8


def community_offsets(key):
    return jax.random.randint(jax.random.fold_in(key, 7), (64, P_SIZE), 1, 9)


def draw_counts(key, part):
    offsets = community_offsets(key)
    member = jax.random.randint(jax.random.fold_in(key, 11), (BATCH,), 0, 64)
    jitter = jax.random.randint(jax.random.fold_in(key, 12), (BATCH, P_SIZE), -1, 2)
    factor = jax.random.randint(jax.random.fold_in(key, 13), (BATCH, P_SIZE), 1, 5)
    exponent = offsets[member] + jitter
    return (factor * jnp.power(2, exponent) - 1).astype(jnp.int32)


def draw_stored(key, part):
    offsets = community_offsets(key)
    member = jax.random.randint(jax.random.fold_in(key, 21), (STORED,), 0, 64)
    spread = 5 * jnp.arange(STORED, dtype=jnp.int32) // STORED
    jitter = jax.random.randint(jax.random.fold_in(key, 22), (STORED, P_SIZE), -spread[:, None], spread[:, None] + 1)
    exponent = jnp.clip(offsets[member] + jitter, 0, 9)
    noise = jax.random.randint(jax.random.fold_in(key, 23), (STORED, P_SIZE), -6, 7)
    levels = 24 * exponent - 108 + noise
    return levels.astype(jnp.float32).astype(jnp.bfloat16)


def draw_scales(key, part):
    position = jnp.arange(STORED, dtype=jnp.float32) / STORED
    jitter = 0.2 * jnp.clip(jax.random.normal(key, (STORED,)), -2.0, 2.0)
    return 0.02888 * jnp.exp(0.2 * position + jitter)


def level_of(stream_key, dims, pieces, low, high):
    def one(axis_at, shards_of):
        steps = jax.random.uniform(jax.random.fold_in(jax.random.fold_in(stream_key, 6), axis_at), (shards_of,), jnp.float32, low / len(pieces), high / len(pieces))
        return jnp.repeat(jnp.exp(steps), dims[axis_at] // shards_of).reshape((-1,) + (1,) * (len(dims) - axis_at - 1))

    loudness = one(*pieces[0])
    for cut in pieces[1:]:
        loudness = loudness * one(*cut)
    return loudness


def bell_draw(rng, shape, scale, most, cuts=(), kind=jnp.bfloat16):
    loudness = level_of(rng, shape, cuts, -0.22, 0.18) if cuts else 1.0
    entries = jax.random.normal(rng, shape, jnp.float32) * scale * loudness
    return jnp.minimum(jnp.maximum(entries, -most), most).astype(kind)


def setup_inputs(seed: int = 0) -> dict:
    key_of = jax.random.split(jax.random.key(seed), 7)
    return {
        "counts": draw_counts(jax.random.fold_in(key_of[6], 71), 0),
        "stored": draw_stored(jax.random.fold_in(key_of[6], 71), 0),
        "scales": draw_scales(jax.random.fold_in(key_of[6], 71), 0),
        "col_means": jnp.clip(0.05 + 0.39999999 * jax.random.uniform(key_of[3], (STORED,), jnp.float32) ** level_of(key_of[3], (STORED,), ((0, 8),), -0.2, 0.2), 0.05, 0.45),
        "eigvecs": bell_draw(key_of[4], (NCOORD, STORED), STORED ** -0.5, 0.03125, ((1, 8),), jnp.float32),
        "eigvals": jnp.clip(jnp.exp(jax.random.uniform(key_of[5], (NCOORD,), jnp.float32, math.log(0.02), math.log(0.2))), 0.02, 0.2),
    }


def reference(counts, stored, scales, col_means, eigvecs, eigvals):
    log_values = jnp.log(counts.astype(jnp.float32) + 0.5)
    centred_log_ratio = (log_values - lax.optimization_barrier(jnp.mean(log_values, axis=1, keepdims=True))).astype(jnp.bfloat16)
    incoming_norm = lax.optimization_barrier(jnp.sum(jnp.square(centred_log_ratio.astype(jnp.float32)), axis=1))

    def step(carry, index):
        projected, sums = carry
        start = (index * STORE_DEV).astype(jnp.int32)
        input_rows = lax.dynamic_slice_in_dim(stored, start, STORE_DEV, 0)
        row_scale_factors = lax.dynamic_slice_in_dim(scales, start, STORE_DEV, 0)
        means = lax.dynamic_slice_in_dim(col_means, start, STORE_DEV, 0)
        vectors = lax.dynamic_slice_in_dim(eigvecs, start, STORE_DEV, 1)
        reference_norm = row_scale_factors * row_scale_factors * lax.optimization_barrier(jnp.sum(jnp.square(input_rows.astype(jnp.float32)), axis=1))
        inner_products = lax.dot_general(centred_log_ratio, input_rows, (((1,), (1,)), ((), ())), preferred_element_type=jnp.float32)
        dist = incoming_norm[:, None] + reference_norm[None, :] - 2.0 * row_scale_factors[None, :] * inner_products
        kernel = jnp.exp(-dist / (2.0 * P_SIZE))
        part = lax.dot_general(kernel - means[None, :], vectors, (((1,), (1,)), ((), ())), precision=lax.Precision.HIGHEST, preferred_element_type=jnp.float32)
        return ((projected + part, sums + lax.optimization_barrier(jnp.sum(kernel, axis=1))), None)
    start_carry = (jnp.zeros((BATCH, NCOORD), jnp.float32), jnp.zeros((BATCH,), jnp.float32))
    (projected, sums), unused = lax.scan(step, start_carry, jnp.arange(N_STORE, dtype=jnp.int32))
    row_mean = sums / STORED
    grand = jnp.sum(col_means) / STORED
    ones_v = lax.optimization_barrier(jnp.sum(eigvecs, axis=1))
    coords = projected + (grand - row_mean)[:, None] * ones_v[None, :]
    return coords / jnp.sqrt(eigvals)[None, :]
```

```python
import functools

import jax
import jax.numpy as jnp
from jax import lax
from jax.experimental import pallas as pl
from jax.experimental.pallas import tpu as pltpu
from jax.sharding import PartitionSpec as P

MESH = pl.DeviceIdType.MESH
LAST = (((1,), (1,)), ((), ()))
CHUNK = 512
NORM_ROWS = 256


def dot_last(left, right):
    return lax.dot_general(left, right, LAST, preferred_element_type=jnp.float32)


def split(value):
    high = value.astype(jnp.bfloat16)
    low = (value - high.astype(jnp.float32)).astype(jnp.bfloat16)
    return high, low


def kernel(
    n,
    counts_hbm,
    stored_hbm,
    scales_hbm,
    means_hbm,
    vectors_hbm,
    out_ref,
    counts,
    stored,
    scales,
    means,
    vectors,
    clr,
    norms,
    pieces,
    message,
    arrived,
    counts_sem,
    stored_sem,
    small_sem,
    clr_send,
    clr_recv,
    sum_send,
    sum_recv,
):
    rows, taxa = counts.shape
    total = stored.shape[0]
    coords = vectors.shape[0]
    chunks = total // CHUNK
    ingest, me = lax.axis_index("ingest"), lax.axis_index("store")

    counts_copy = pltpu.make_async_copy(counts_hbm, counts, counts_sem)
    counts_copy.start()
    small = [
        pltpu.make_async_copy(source, target, small_sem.at[i])
        for i, (source, target) in enumerate(
            ((scales_hbm, scales), (means_hbm, means), (vectors_hbm, vectors))
        )
    ]
    for copy in small:
        copy.start()

    def stored_copy(c):
        at = pl.ds(c * CHUNK, CHUNK)
        return pltpu.make_async_copy(stored_hbm.at[at], stored.at[at], stored_sem.at[c])

    for c in range(chunks):
        stored_copy(c).start()

    barrier = pltpu.get_barrier_semaphore()
    for k in range(1, n):
        pl.semaphore_signal(
            barrier, inc=1, device_id=(ingest, lax.rem(me + k, n)), device_id_type=MESH
        )

    counts_copy.wait()
    logs = jnp.log(counts[...].astype(jnp.float32) + 0.5)
    clr[0] = (logs - jnp.mean(logs, axis=1, keepdims=True)).astype(jnp.bfloat16)
    pl.semaphore_wait(barrier, n - 1)

    gathers = [
        pltpu.make_async_remote_copy(
            src_ref=clr.at[0],
            dst_ref=clr.at[k],
            send_sem=clr_send.at[k],
            recv_sem=clr_recv.at[k],
            device_id=(ingest, lax.rem(me + k, n)),
            device_id_type=MESH,
        )
        for k in range(1, n)
    ]
    for copy in gathers:
        copy.start()

    for copy in small:
        copy.wait()
    ones = jnp.ones((8, CHUNK), jnp.bfloat16)

    def prepare(c, ones_v):
        stored_copy(c).wait()
        for r in range(CHUNK // NORM_ROWS):
            at = pl.multiple_of(c * CHUNK + r * NORM_ROWS, NORM_ROWS)
            squares = jnp.zeros((NORM_ROWS, 128), jnp.float32)
            for t in range(taxa // 128):
                level = stored[pl.ds(at, NORM_ROWS), t * 128 : (t + 1) * 128].astype(jnp.float32)
                squares += level * level
            both = jnp.concatenate(split(squares), axis=1)
            sums = dot_last(ones[:, :256], both)
            scale = scales[:, pl.ds(at, NORM_ROWS)]
            norms[:, pl.ds(at, NORM_ROWS)] = sums[:1] * (scale * scale)
        at = pl.ds(pl.multiple_of(c * CHUNK, CHUNK), CHUNK)
        high, low = split(vectors[:, at])
        pieces[:coords, at] = high
        pieces[coords:, at] = low
        return ones_v + dot_last(ones, pieces[:, at])

    ones_v = lax.fori_loop(0, chunks, prepare, jnp.zeros((8, 2 * coords), jnp.float32))

    for copy in gathers:
        copy.wait()

    batch = n * rows
    samples = clr[...].reshape(batch, taxa)
    new_norm = jnp.zeros((batch, 128), jnp.float32)
    for t in range(taxa // 128):
        piece = samples[:, t * 128 : (t + 1) * 128].astype(jnp.float32)
        new_norm += piece * piece
    new_norm = jnp.sum(new_norm, axis=1, keepdims=True)

    def step(c, carry):
        sums, projected = carry
        at = pl.ds(pl.multiple_of(c * CHUNK, CHUNK), CHUNK)
        dots = dot_last(clr[...].reshape(batch, taxa), stored[at, :])
        dist = new_norm + norms[:, at] - 2.0 * scales[:, at] * dots
        value = jnp.exp(dist * (-0.5 / taxa)) - means[:, at]
        for t in range(CHUNK // 128):
            sums += value[:, t * 128 : (t + 1) * 128]
        projected += dot_last(jnp.concatenate(split(value), axis=0), pieces[:, at])
        return sums, projected

    sums, projected = lax.fori_loop(
        0,
        chunks,
        step,
        (jnp.zeros((batch, 128), jnp.float32), jnp.zeros((2 * batch, 2 * coords), jnp.float32)),
    )

    def fold(value):
        return value[:, :coords] + value[:, coords:]

    projected = fold(projected[:batch] + projected[batch:])
    sums = jnp.sum(sums, axis=1, keepdims=True)
    message[:, :rows, :coords] = projected.reshape(n, rows, coords)
    message[:, :rows, coords:] = jnp.broadcast_to(sums, (batch, coords)).reshape(n, rows, coords)
    message[:, rows:, :coords] = jnp.broadcast_to(fold(ones_v)[None], (n, 8, coords))
    message[:, rows:, coords:] = jnp.zeros((n, 8, coords), jnp.float32)

    scatters = [
        pltpu.make_async_remote_copy(
            src_ref=message.at[k],
            dst_ref=arrived.at[k],
            send_sem=sum_send.at[k],
            recv_sem=sum_recv.at[k],
            device_id=(ingest, lax.rem(me + n - k, n)),
            device_id_type=MESH,
        )
        for k in range(1, n)
    ]
    for copy in scatters:
        copy.start()
    whole = message[0]
    for copy in scatters:
        copy.wait()
    for k in range(1, n):
        whole += arrived[k]
    mean = whole[:rows, coords:] * (1.0 / (total * n))
    out_ref[...] = whole[:rows, :coords] - mean * whole[rows : rows + 1, :coords]


def on_device(n, counts, stored, scales, col_means, eigvecs, eigvals):
    rows, taxa = counts.shape
    total = stored.shape[0]
    coords = eigvecs.shape[0]
    chunks = total // CHUNK
    result = pl.pallas_call(
        functools.partial(kernel, n),
        out_shape=jax.ShapeDtypeStruct((rows, coords), jnp.float32),
        in_specs=[pl.BlockSpec(memory_space=pl.ANY)] * 5,
        out_specs=pl.BlockSpec(memory_space=pltpu.VMEM),
        scratch_shapes=[
            pltpu.VMEM((rows, taxa), jnp.int32),
            pltpu.VMEM((total, taxa), jnp.bfloat16),
            pltpu.VMEM((1, total), jnp.float32),
            pltpu.VMEM((1, total), jnp.float32),
            pltpu.VMEM((coords, total), jnp.float32),
            pltpu.VMEM((n, rows, taxa), jnp.bfloat16),
            pltpu.VMEM((1, total), jnp.float32),
            pltpu.VMEM((2 * coords, total), jnp.bfloat16),
            pltpu.VMEM((n, rows + 8, 2 * coords), jnp.float32),
            pltpu.VMEM((n, rows + 8, 2 * coords), jnp.float32),
            pltpu.SemaphoreType.DMA,
            pltpu.SemaphoreType.DMA((chunks,)),
            pltpu.SemaphoreType.DMA((3,)),
            pltpu.SemaphoreType.DMA((n,)),
            pltpu.SemaphoreType.DMA((n,)),
            pltpu.SemaphoreType.DMA((n,)),
            pltpu.SemaphoreType.DMA((n,)),
        ],
        compiler_params=pltpu.CompilerParams(
            collective_id=0, has_side_effects=True, vmem_limit_bytes=50 * 1024 * 1024
        ),
    )(counts, stored, scales.reshape(1, -1), col_means.reshape(1, -1), eigvecs)
    return result / jnp.sqrt(eigvals)[None, :]


def solution(mesh):
    in_specs = (
        P(("ingest", "store"), None),
        P("store", None),
        P("store"),
        P("store"),
        P(None, "store"),
        P(),
    )
    out_specs = P(("ingest", "store"), None)
    return jax.shard_map(
        functools.partial(on_device, mesh.shape["store"]),
        mesh=mesh,
        in_specs=in_specs,
        out_specs=out_specs,
        check_vma=False,
    )
```

```python
import functools

import jax
import jax.numpy as jnp
from jax import lax
from jax.experimental import pallas as pl
from jax.experimental.pallas import tpu as pltpu
from jax.sharding import PartitionSpec as P

MESH = pl.DeviceIdType.MESH
LAST = (((1,), (1,)), ((), ()))
CHUNK = 1024
NORM_ROWS = 256


def dot_last(left, right):
    return lax.dot_general(left, right, LAST, preferred_element_type=jnp.float32)


def split(value):
    high = value.astype(jnp.bfloat16)
    low = (value - high.astype(jnp.float32)).astype(jnp.bfloat16)
    return high, low


def kernel(
    n,
    counts_hbm,
    stored_hbm,
    scales_hbm,
    means_hbm,
    vectors_hbm,
    values_hbm,
    out_ref,
    counts,
    stored,
    scales,
    means,
    vectors,
    values,
    clr,
    norms,
    pieces,
    ones_sums,
    message,
    arrived,
    counts_sem,
    stored_sem,
    small_sem,
    clr_send,
    clr_recv,
    ones_send,
    ones_recv,
    sum_send,
    sum_recv,
):
    rows, taxa = counts.shape
    total = stored.shape[0]
    coords = vectors.shape[0]
    chunks = total // CHUNK
    ingest, me = lax.axis_index("ingest"), lax.axis_index("store")

    counts_copy = pltpu.make_async_copy(counts_hbm, counts, counts_sem)
    counts_copy.start()
    local = [
        pltpu.make_async_copy(source, target, small_sem.at[i])
        for i, (source, target) in enumerate(
            ((vectors_hbm, vectors), (scales_hbm, scales), (means_hbm, means), (values_hbm, values))
        )
    ]
    for copy in local:
        copy.start()

    def stored_copy(c):
        at = pl.ds(c * CHUNK, CHUNK)
        return pltpu.make_async_copy(stored_hbm.at[at], stored.at[at], stored_sem.at[c])


    barrier = pltpu.get_barrier_semaphore()
    for k in range(1, n):
        pl.semaphore_signal(
            barrier, inc=1, device_id=(ingest, lax.rem(me + k, n)), device_id_type=MESH
        )

    counts_copy.wait()
    for c in range(chunks):
        stored_copy(c).start()
    logs = jnp.log(counts[...].astype(jnp.float32) + 0.5)
    clr[0] = (logs - jnp.mean(logs, axis=1, keepdims=True)).astype(jnp.bfloat16)

    pl.semaphore_wait(barrier, n - 1)

    def to_all(source, target, send, recv, sign):
        return [
            pltpu.make_async_remote_copy(
                src_ref=source(k),
                dst_ref=target.at[k],
                send_sem=send.at[k],
                recv_sem=recv.at[k],
                device_id=(ingest, lax.rem(me + n + sign * k, n)),
                device_id_type=MESH,
            )
            for k in range(1, n)
        ]

    gathers = to_all(lambda k: clr.at[0], clr, clr_send, clr_recv, 1)
    for copy in gathers:
        copy.start()

    ones = jnp.ones((8, CHUNK), jnp.bfloat16)
    local[0].wait()
    ones_v = jnp.zeros((8, 2 * coords), jnp.float32)
    for c in range(chunks):
        at = slice(c * CHUNK, (c + 1) * CHUNK)
        high, low = split(vectors[:, at])
        pieces[:coords, at] = high
        pieces[coords:, at] = low
        ones_v += dot_last(ones, pieces[:, at])
    ones_sums[0] = ones_v
    shares = to_all(lambda k: ones_sums.at[0], ones_sums, ones_send, ones_recv, 1)
    for copy in shares:
        copy.start()

    for copy in local[1:]:
        copy.wait()

    def prepare(r, unused):
        at = pl.multiple_of(r * NORM_ROWS, NORM_ROWS)
        squares = jnp.zeros((NORM_ROWS, 128), jnp.float32)
        for t in range(taxa // 128):
            level = stored[pl.ds(at, NORM_ROWS), t * 128 : (t + 1) * 128].astype(jnp.float32)
            squares += level * level
        sums = dot_last(ones[:, :256], jnp.concatenate(split(squares), axis=1))
        scale = scales[:, pl.ds(at, NORM_ROWS)]
        norms[:, pl.ds(at, NORM_ROWS)] = sums[:1] * (scale * scale)
        return unused

    per = CHUNK // NORM_ROWS
    for c in range(chunks):
        stored_copy(c).wait()
        lax.fori_loop(c * per, (c + 1) * per, prepare, 0)

    for copy in gathers:
        copy.wait()

    batch = n * rows
    samples = clr[...].reshape(batch, taxa)
    new_norm = jnp.zeros((batch, 128), jnp.float32)
    for t in range(taxa // 128):
        piece = samples[:, t * 128 : (t + 1) * 128].astype(jnp.float32)
        new_norm += piece * piece
    new_norm = jnp.sum(new_norm, axis=1, keepdims=True)

    def step(c, carry):
        sums, projected = carry
        at = slice(c * CHUNK, (c + 1) * CHUNK)
        dots = dot_last(clr[...].reshape(batch, taxa), stored[at, :])
        dist = new_norm + norms[:, at] - 2.0 * scales[:, at] * dots
        value = jnp.exp(dist * (-0.5 / taxa)) - means[:, at]
        for t in range(CHUNK // 128):
            sums += value[:, t * 128 : (t + 1) * 128]
        projected += dot_last(jnp.concatenate(split(value), axis=0), pieces[:, at])
        return sums, projected

    carry = (
        jnp.zeros((batch, 128), jnp.float32),
        jnp.zeros((2 * batch, 2 * coords), jnp.float32),
    )
    for c in range(chunks):
        carry = step(c, carry)
    sums, projected = carry

    def fold(value):
        return value[:, :coords] + value[:, coords:]

    for copy in shares:
        copy.wait()
    ones_v = ones_sums[0]
    for k in range(1, n):
        ones_v += ones_sums[k]
    ones_v = fold(ones_v)[:1] * (1.0 / (total * n))
    projected = fold(projected[:batch] + projected[batch:])
    projected -= jnp.sum(sums, axis=1, keepdims=True) * ones_v
    projected = projected.reshape(n, 2, rows // 2, coords)
    message[:, :, :coords] = projected[:, 0]
    message[:, :, coords:] = projected[:, 1]

    scatters = to_all(lambda k: message.at[k], arrived, sum_send, sum_recv, -1)
    for copy in scatters:
        copy.start()
    whole = message[0]
    for k, copy in enumerate(scatters, 1):
        copy.wait_recv()
        whole += arrived[k]
    root = jnp.sqrt(values[...])
    out_ref[: rows // 2, :] = whole[:, :coords] / root
    out_ref[rows // 2 :, :] = whole[:, coords:] / root
    for copy in scatters:
        copy.wait_send()


def on_device(n, counts, stored, scales, col_means, eigvecs, eigvals):
    rows, taxa = counts.shape
    total = stored.shape[0]
    coords = eigvecs.shape[0]
    chunks = total // CHUNK
    return pl.pallas_call(
        functools.partial(kernel, n),
        out_shape=jax.ShapeDtypeStruct((rows, coords), jnp.float32),
        in_specs=[pl.BlockSpec(memory_space=pltpu.HBM)] * 6,
        out_specs=pl.BlockSpec(memory_space=pltpu.VMEM),
        scratch_shapes=[
            pltpu.VMEM((rows, taxa), jnp.int32),
            pltpu.VMEM((total, taxa), jnp.bfloat16),
            pltpu.VMEM((1, total), jnp.float32),
            pltpu.VMEM((1, total), jnp.float32),
            pltpu.VMEM((coords, total), jnp.float32),
            pltpu.VMEM((1, coords), jnp.float32),
            pltpu.VMEM((n, rows, taxa), jnp.bfloat16),
            pltpu.VMEM((1, total), jnp.float32),
            pltpu.VMEM((2 * coords, total), jnp.bfloat16),
            pltpu.VMEM((n, 8, 2 * coords), jnp.float32),
            pltpu.VMEM((n, rows // 2, 2 * coords), jnp.float32),
            pltpu.VMEM((n, rows // 2, 2 * coords), jnp.float32),
            pltpu.SemaphoreType.DMA,
            pltpu.SemaphoreType.DMA((chunks,)),
            pltpu.SemaphoreType.DMA((4,)),
            pltpu.SemaphoreType.DMA((n,)),
            pltpu.SemaphoreType.DMA((n,)),
            pltpu.SemaphoreType.DMA((n,)),
            pltpu.SemaphoreType.DMA((n,)),
            pltpu.SemaphoreType.DMA((n,)),
            pltpu.SemaphoreType.DMA((n,)),
        ],
        compiler_params=pltpu.CompilerParams(
            collective_id=0, has_side_effects=True, vmem_limit_bytes=64 * 1024 * 1024
        ),
    )(counts, stored, scales.reshape(1, -1), col_means.reshape(1, -1), eigvecs, eigvals.reshape(1, -1))


def solution(mesh):
    in_specs = (
        P(("ingest", "store"), None),
        P("store", None),
        P("store"),
        P("store"),
        P(None, "store"),
        P(),
    )
    out_specs = P(("ingest", "store"), None)
    return jax.shard_map(
        functools.partial(on_device, mesh.shape["store"]),
        mesh=mesh,
        in_specs=in_specs,
        out_specs=out_specs,
        check_vma=False,
    )
```

```python
import functools

import jax
import jax.numpy as jnp
from jax import lax
from jax.experimental import pallas as pl
from jax.experimental.pallas import tpu as pltpu
from jax.sharding import PartitionSpec as P

MESH = pl.DeviceIdType.MESH
LAST = (((1,), (1,)), ((), ()))
CHUNK = 1024
NORM_ROWS = 256


def dot_last(left, right):
    return lax.dot_general(left, right, LAST, preferred_element_type=jnp.float32)


def split(value):
    high = value.astype(jnp.bfloat16)
    low = (value - high.astype(jnp.float32)).astype(jnp.bfloat16)
    return high, low


def kernel(
    n,
    counts_hbm,
    stored_hbm,
    scales_hbm,
    means_hbm,
    vectors_hbm,
    values_hbm,
    out_ref,
    counts,
    stored,
    scales,
    means,
    vectors,
    values,
    clr,
    norms,
    pieces,
    ones_sums,
    message,
    arrived,
    counts_sem,
    stored_sem,
    small_sem,
    clr_send,
    clr_recv,
    ones_send,
    ones_recv,
    sum_send,
    sum_recv,
):
    rows, taxa = counts.shape
    total = stored.shape[0]
    coords = vectors.shape[0]
    chunks = total // CHUNK
    ingest, me = lax.axis_index("ingest"), lax.axis_index("store")

    def partner(k):
        place, bit = 0, 1
        while bit < n:
            place = place + bit * lax.rem(me // bit + k // bit, 2)
            bit *= 2
        return place

    slots = range(n - 1, 0, -1)
    partners = {k: (ingest, partner(k)) for k in slots}

    counts_copy = pltpu.make_async_copy(counts_hbm, counts, counts_sem)
    counts_copy.start()
    barrier = pltpu.get_barrier_semaphore()
    for k in slots:
        pl.semaphore_signal(barrier, inc=1, device_id=partners[k], device_id_type=MESH)

    local = [
        pltpu.make_async_copy(source, target, small_sem.at[i])
        for i, (source, target) in enumerate(
            ((vectors_hbm, vectors), (scales_hbm, scales), (means_hbm, means), (values_hbm, values))
        )
    ]
    for copy in local:
        copy.start()

    def stored_copy(c):
        at = pl.ds(c * CHUNK, CHUNK)
        return pltpu.make_async_copy(stored_hbm.at[at], stored.at[at], stored_sem.at[c])

    counts_copy.wait()
    for c in range(chunks):
        stored_copy(c).start()
    logs = jnp.log(counts[...].astype(jnp.float32) + 0.5)
    clr[0] = (logs - jnp.mean(logs, axis=1, keepdims=True)).astype(jnp.bfloat16)

    pl.semaphore_wait(barrier, n - 1)

    def to_all(source, target, send, recv):
        return [
            pltpu.make_async_remote_copy(
                src_ref=source(k),
                dst_ref=target.at[k],
                send_sem=send.at[k],
                recv_sem=recv.at[k],
                device_id=partners[k],
                device_id_type=MESH,
            )
            for k in slots
        ]

    gathers = to_all(lambda k: clr.at[0], clr, clr_send, clr_recv)
    for copy in gathers:
        copy.start()

    ones = jnp.ones((8, CHUNK), jnp.bfloat16)
    local[0].wait()
    ones_v = jnp.zeros((8, 2 * coords), jnp.float32)
    for c in range(chunks):
        at = slice(c * CHUNK, (c + 1) * CHUNK)
        high, low = split(vectors[:, at])
        pieces[:coords, at] = high
        pieces[coords:, at] = low
        ones_v += dot_last(ones, pieces[:, at])
    ones_sums[0] = ones_v
    shares = to_all(lambda k: ones_sums.at[0], ones_sums, ones_send, ones_recv)
    for copy in shares:
        copy.start()

    for copy in local[1:]:
        copy.wait()

    def prepare(r, unused):
        at = pl.multiple_of(r * NORM_ROWS, NORM_ROWS)
        squares = jnp.zeros((NORM_ROWS, 128), jnp.float32)
        for t in range(taxa // 128):
            level = stored[pl.ds(at, NORM_ROWS), t * 128 : (t + 1) * 128].astype(jnp.float32)
            squares += level * level
        sums = dot_last(ones[:, :256], jnp.concatenate(split(squares), axis=1))
        scale = scales[:, pl.ds(at, NORM_ROWS)]
        norms[:, pl.ds(at, NORM_ROWS)] = sums[:1] * (scale * scale)
        return unused

    per = CHUNK // NORM_ROWS
    early = chunks - 1
    for c in range(early):
        stored_copy(c).wait()
        lax.fori_loop(c * per, (c + 1) * per, prepare, 0)

    for c in range(early, chunks):
        stored_copy(c).wait()
    inverse = 1.0 / jnp.sqrt(values[...])
    for copy in gathers:
        copy.wait_recv()

    batch = n * rows
    samples = clr[...].reshape(batch, taxa)
    new_norm = jnp.zeros((batch, 128), jnp.float32)
    for t in range(taxa // 128):
        piece = samples[:, t * 128 : (t + 1) * 128].astype(jnp.float32)
        new_norm += piece * piece
    new_norm = jnp.sum(new_norm, axis=1, keepdims=True)

    def step(c, carry):
        sums, projected = carry
        at = slice(c * CHUNK, (c + 1) * CHUNK)
        dots = dot_last(clr[...].reshape(batch, taxa), stored[at, :])
        dist = new_norm + norms[:, at] - 2.0 * scales[:, at] * dots
        value = jnp.exp(dist * (-0.5 / taxa)) - means[:, at]
        for t in range(CHUNK // 128):
            sums += value[:, t * 128 : (t + 1) * 128]
        projected += dot_last(jnp.concatenate(split(value), axis=0), pieces[:, at])
        return sums, projected

    carry = (
        jnp.zeros((batch, 128), jnp.float32),
        jnp.zeros((2 * batch, 2 * coords), jnp.float32),
    )
    for c in range(chunks):
        if c >= early:
            for r in range(c * per, (c + 1) * per):
                prepare(r, 0)
        carry = step(c, carry)
    sums, projected = carry

    def fold(value):
        return value[:, :coords] + value[:, coords:]

    for copy in shares:
        copy.wait_recv()
    ones_v = ones_sums[0]
    for k in range(1, n):
        ones_v += ones_sums[k]
    ones_v = fold(ones_v)[:1] * (1.0 / (total * n))
    projected = fold(projected[:batch] + projected[batch:])
    projected -= jnp.sum(sums, axis=1, keepdims=True) * ones_v
    projected = projected.reshape(n, 2, rows // 2, coords)
    message[:, :, :coords] = projected[:, 0]
    message[:, :, coords:] = projected[:, 1]

    scatters = to_all(lambda k: message.at[k], arrived, sum_send, sum_recv)
    for copy in scatters:
        copy.start()
    for copy in gathers + shares:
        copy.wait_send()
    whole = message[0]
    for copy in reversed(scatters):
        copy.wait_recv()
    for k in slots:
        whole += arrived[k]
    out_ref[: rows // 2, :] = whole[:, :coords] * inverse
    out_ref[rows // 2 :, :] = whole[:, coords:] * inverse
    for copy in scatters:
        copy.wait_send()


def on_device(n, counts, stored, scales, col_means, eigvecs, eigvals):
    rows, taxa = counts.shape
    total = stored.shape[0]
    coords = eigvecs.shape[0]
    chunks = total // CHUNK
    return pl.pallas_call(
        functools.partial(kernel, n),
        out_shape=jax.ShapeDtypeStruct((rows, coords), jnp.float32),
        in_specs=[pl.BlockSpec(memory_space=pltpu.HBM)] * 6,
        out_specs=pl.BlockSpec(memory_space=pltpu.VMEM),
        scratch_shapes=[
            pltpu.VMEM((rows, taxa), jnp.int32),
            pltpu.VMEM((total, taxa), jnp.bfloat16),
            pltpu.VMEM((1, total), jnp.float32),
            pltpu.VMEM((1, total), jnp.float32),
            pltpu.VMEM((coords, total), jnp.float32),
            pltpu.VMEM((1, coords), jnp.float32),
            pltpu.VMEM((n, rows, taxa), jnp.bfloat16),
            pltpu.VMEM((1, total), jnp.float32),
            pltpu.VMEM((2 * coords, total), jnp.bfloat16),
            pltpu.VMEM((n, 8, 2 * coords), jnp.float32),
            pltpu.VMEM((n, rows // 2, 2 * coords), jnp.float32),
            pltpu.VMEM((n, rows // 2, 2 * coords), jnp.float32),
            pltpu.SemaphoreType.DMA,
            pltpu.SemaphoreType.DMA((chunks,)),
            pltpu.SemaphoreType.DMA((4,)),
            pltpu.SemaphoreType.DMA((n,)),
            pltpu.SemaphoreType.DMA((n,)),
            pltpu.SemaphoreType.DMA((n,)),
            pltpu.SemaphoreType.DMA((n,)),
            pltpu.SemaphoreType.DMA((n,)),
            pltpu.SemaphoreType.DMA((n,)),
        ],
        compiler_params=pltpu.CompilerParams(
            collective_id=0, has_side_effects=True, vmem_limit_bytes=64 * 1024 * 1024
        ),
    )(counts, stored, scales.reshape(1, -1), col_means.reshape(1, -1), eigvecs, eigvals.reshape(1, -1))


def solution(mesh):
    in_specs = (
        P(("ingest", "store"), None),
        P("store", None),
        P("store"),
        P("store"),
        P(None, "store"),
        P(),
    )
    out_specs = P(("ingest", "store"), None)
    return jax.shard_map(
        functools.partial(on_device, mesh.shape["store"]),
        mesh=mesh,
        in_specs=in_specs,
        out_specs=out_specs,
        check_vma=False,
    )
```
